32 devices in a mesh: dp: 16 (over z, y, core), tensor: 2 (over x).
Axes of the slice: x: 2, y: 2, z: 4, core: 2. Of those that a mesh axis runs over, the one named last changes fastest.
Arguments:
- clip_feats: bfloat16 [2048, 1280], P('dp', 'tensor'), may hold values from -3 to 3
- proj_weight: bfloat16 [1280, 512], P('tensor'), may hold values from -1 to 1
- caption_emb: bfloat16 [2048, 512], P(('dp', 'tensor')), may hold values from -1.25 to 1.25
- logit_scale: float32 [1], replicated, may hold values from 20 to 400
- pair_perm: int32 [2048], replicated, may hold values from 0 to 2047, as said below
Outputs:
- clip_grad: float32 [2048, 1280], P('dp', 'tensor')
- caption_grad: float32 [2048, 512], P(('dp', 'tensor'))
- row_loss: float32 [2048], P('dp')
The draws below stay inside these ranges and needn't reach their ends.
Inputs may be any that keep to these rules, and one draw needn't show every extreme that they name: pair_perm is a permutation of the 2048 caption indices.
All inputs are finite; a program needn't handle non-finite values.
Results may differ from the reference program's by a relative error of at most 0.012.
The reference program's roundings to bfloat16 on the way (of `videos`, `captions`, `weights` and `raw_grad`) count: a program that leaves them out, or rounds other values in their place, can miss the bound.
Values may be sent and summed in bfloat16 or wider, within the bound.
A program may use at most 64 MiB of HBM per device.

```python
import math
import jax
import jax.numpy as jnp
from jax import lax

DV = 1280
E = 512
B = 2048


def shared_draw(key):
    pair_order = jax.random.permutation(jax.random.fold_in(key, 11), B).astype(jnp.int32)
    clip_base = jnp.clip(jax.random.normal(jax.random.fold_in(key, 12), (B, DV), jnp.float32), -6.0, 6.0) * 0.05
    proj_base = jnp.clip(jax.random.normal(jax.random.fold_in(key, 13), (DV, E), jnp.float32), -4.0, 4.0) / math.sqrt(DV)
    cap_base = jnp.clip(jax.random.normal(jax.random.fold_in(key, 14), (B, E), jnp.float32), -6.0, 6.0) * 0.05
    logit_value = jnp.exp(jax.random.uniform(jax.random.fold_in(key, 17), (1,), jnp.float32, math.log(20.0), math.log(100.0)))
    clip_feats = clip_base.astype(jnp.bfloat16)
    proj_weight = proj_base.astype(jnp.bfloat16)
    caption = cap_base
    return (clip_feats, proj_weight, caption.astype(jnp.bfloat16), logit_value, pair_order)


def draw_clip_feats(key, part):
    return shared_draw(key)[0]


def draw_proj_weight(key, part):
    return shared_draw(key)[1]


def draw_caption_emb(key, part):
    return shared_draw(key)[2]


def draw_logit_scale(key, part):
    return shared_draw(key)[3]


def draw_pair_perm(key, part):
    return shared_draw(key)[4]


def setup_inputs(seed: int = 0) -> dict:
    seeds = jax.random.split(jax.random.key(seed), 6)
    clip_feats = draw_clip_feats(jax.random.fold_in(seeds[5], 71), 0)
    proj_weight = draw_proj_weight(jax.random.fold_in(seeds[5], 71), 0)
    caption_emb = draw_caption_emb(jax.random.fold_in(seeds[5], 71), 0)
    logit_scale = draw_logit_scale(jax.random.fold_in(seeds[5], 71), 0)
    pair_perm = draw_pair_perm(jax.random.fold_in(seeds[5], 71), 0)
    return {"clip_feats": clip_feats, "proj_weight": proj_weight, "caption_emb": caption_emb, "logit_scale": logit_scale, "pair_perm": pair_perm}


norm_eps = 1e-06

def unit_rows(values):
    squares = lax.optimization_barrier(jnp.sum(values * values, axis=1, keepdims=True))
    inverse = lax.rsqrt(squares + norm_eps)
    return (values * inverse, inverse)

def reference(clip_feats, proj_weight, caption_emb, logit_scale, pair_perm):
    logit = logit_scale[0]
    raw_proj = jnp.dot(clip_feats, proj_weight, preferred_element_type=jnp.float32)
    unit_vid, vid_inv = unit_rows(raw_proj)
    videos = unit_vid.astype(jnp.bfloat16)
    cap_unit, cap_inv = unit_rows(caption_emb.astype(jnp.float32))
    captions = cap_unit.astype(jnp.bfloat16)
    row_count = videos.shape[0]
    width = captions.shape[1]
    row_block = math.gcd(row_count, 2048)
    block_count = row_count // row_block
    col_ids = jnp.arange(row_count, dtype=jnp.int32)

    def advance(cap_acc, block_index):
        offset = block_index * row_block
        vid_rows = lax.dynamic_slice_in_dim(videos, offset, row_block, 0)
        wanted = lax.dynamic_slice_in_dim(pair_perm, offset, row_block, 0)
        scores = logit * lax.dot_general(vid_rows, captions, (((1,), (1,)), ((), ())), preferred_element_type=jnp.float32)
        onehot = (col_ids[None, :] == wanted[:, None]).astype(jnp.float32)
        row_top = lax.optimization_barrier(jnp.max(scores, axis=1, keepdims=True))
        totals = lax.optimization_barrier(jnp.sum(jnp.exp(scores - row_top), axis=1, keepdims=True))
        positive = lax.optimization_barrier(jnp.sum(scores * onehot, axis=1))
        losses = row_top[:, 0] + jnp.log(totals[:, 0]) - positive
        weights = (jnp.exp(scores - row_top) / totals - onehot).astype(jnp.bfloat16)
        vid_grad = logit * jnp.dot(weights, captions, preferred_element_type=jnp.float32)
        cap_acc = cap_acc + logit * lax.dot_general(weights, vid_rows, (((0,), (0,)), ((), ())), preferred_element_type=jnp.float32)
        return (cap_acc, (losses, vid_grad))
    cap_grad, (losses, vid_grad) = lax.scan(advance, jnp.zeros((row_count, width), jnp.float32), jnp.arange(block_count, dtype=jnp.int32))
    losses = losses.reshape(row_count)
    vid_grad = vid_grad.reshape(row_count, width)
    vid_dot = lax.optimization_barrier(jnp.sum(unit_vid * vid_grad, axis=1, keepdims=True))
    raw_grad = ((vid_grad - unit_vid * vid_dot) * vid_inv).astype(jnp.bfloat16)
    clip_grad = lax.dot_general(raw_grad, proj_weight, (((1,), (1,)), ((), ())), preferred_element_type=jnp.float32)
    cap_dot = lax.optimization_barrier(jnp.sum(cap_unit * cap_grad, axis=1, keepdims=True))
    caption_grad = (cap_grad - cap_unit * cap_dot) * cap_inv
    return (clip_grad, caption_grad, losses)
```

```python
import functools

import jax
import jax.numpy as jnp
from jax import lax
from jax.experimental import pallas as pl
from jax.experimental.pallas import tpu as pltpu
from jax.sharding import PartitionSpec as P

norm_eps = 1e-06
MESH = pl.DeviceIdType.MESH
f32 = jnp.float32
bf16 = jnp.bfloat16


def inner_size(dp):
    return max(n for n in range(1, dp + 1) if dp % n == 0 and n * n <= dp)


def kernel(
    dp,
    tensor,
    logit_ref,
    perm_ref,
    clip_hbm,
    proj_hbm,
    cap_hbm,
    clip_grad_ref,
    cap_grad_ref,
    loss_ref,
    clip_v,
    proj_v,
    cap_v,
    part_send,
    part_recv,
    caps,
    vids,
    stats,
    loss_v,
    vid_send,
    vid_recv,
    cap_send,
    cap_recv,
    raw_all,
    load_sem,
    part_ss,
    part_rs,
    caps_ss,
    caps_rs,
    vids_ss,
    vids_rs,
    stats_ss,
    stats_rs,
    vg_ss,
    vg_rs,
    cg_ss,
    cg_rs,
    raw_ss,
    raw_rs,
):
    inner = inner_size(dp)
    na = dp // inner
    nb = inner * tensor
    rows, feats = clip_v.shape
    vrow = rows // tensor
    ccol, width = cap_v.shape
    d = lax.axis_index("dp")
    t = lax.axis_index("tensor")
    a = lax.div(d, inner)
    i = lax.rem(d, inner)
    b = i * tensor + t

    def row_peer(k):
        pb = lax.rem(b + k, nb)
        return pb, (a * inner + lax.div(pb, tensor), lax.rem(pb, tensor))

    def col_peer(k):
        pa = lax.rem(a + k, na)
        return pa, (pa * inner + i, t)

    def tensor_peer(k):
        pt = lax.rem(t + k, tensor)
        return pt, (d, pt)

    def remote(src, dst, ss, rs, device):
        return pltpu.make_async_remote_copy(
            src_ref=src, dst_ref=dst, send_sem=ss, recv_sem=rs, device_id=device, device_id_type=MESH
        )

    load_clip = pltpu.make_async_copy(clip_hbm, clip_v, load_sem.at[0])
    load_proj = pltpu.make_async_copy(proj_hbm, proj_v, load_sem.at[1])
    load_cap = pltpu.make_async_copy(cap_hbm, cap_v, load_sem.at[2])
    load_clip.start()
    load_proj.start()
    load_cap.start()
    barrier = pltpu.get_barrier_semaphore()
    for k in range(1, nb):
        pl.semaphore_signal(barrier, inc=1, device_id=row_peer(k)[1], device_id_type=MESH)
    for k in range(1, na):
        pl.semaphore_signal(barrier, inc=1, device_id=col_peer(k)[1], device_id_type=MESH)

    logit = logit_ref[0]
    sends = []

    load_clip.wait()
    load_proj.wait()
    part_send[...] = jnp.dot(clip_v[...], proj_v[...], preferred_element_type=f32).reshape(tensor, vrow, width)
    pl.semaphore_wait(barrier, nb + na - 2)
    part_copies = []
    for k in range(1, tensor):
        pt, dev = tensor_peer(k)
        c = remote(part_send.at[pt], part_recv.at[k - 1], part_ss.at[k - 1], part_rs.at[k - 1], dev)
        c.start()
        part_copies.append(c)

    load_cap.wait()
    cap_f = cap_v[...].astype(f32)
    cap_inv = lax.rsqrt(jnp.sum(cap_f * cap_f, axis=1, keepdims=True) + norm_eps)
    caps[a] = (cap_f * cap_inv).astype(bf16)
    cap_copies = []
    for k in range(1, na):
        pa, dev = col_peer(k)
        c = remote(caps.at[a], caps.at[a], caps_ss.at[k - 1], caps_rs.at[k - 1], dev)
        c.start()
        cap_copies.append(c)

    raw_proj = part_send[t]
    for k in range(1, tensor):
        part_copies[k - 1].wait_recv()
        raw_proj = raw_proj + part_recv[k - 1]
    vid_inv = lax.rsqrt(jnp.sum(raw_proj * raw_proj, axis=1, keepdims=True) + norm_eps)
    unit_vid = raw_proj * vid_inv
    vids[b] = unit_vid.astype(bf16)
    vid_copies = []
    for k in range(1, nb):
        pb, dev = row_peer(k)
        c = remote(vids.at[b], vids.at[b], vids_ss.at[k - 1], vids_rs.at[k - 1], dev)
        c.start()
        vid_copies.append(c)
    for c in cap_copies:
        c.wait_recv()
    for c in vid_copies:
        c.wait_recv()

    captions = caps[...].reshape(na * ccol, width)
    videos = vids[...].reshape(nb * vrow, width)
    tile_rows = nb * vrow
    scores = logit * lax.dot_general(captions, videos, (((1,), (1,)), ((), ())), preferred_element_type=f32)
    wanted = perm_ref[:, pl.ds(pl.multiple_of(a * tile_rows, tile_rows), tile_rows)]
    index = lax.broadcasted_iota(jnp.int32, (na * ccol, 1), 0)
    column = (index // ccol) * (nb * ccol) + b * ccol + index % ccol
    hit = column == wanted
    top = jnp.max(scores, axis=0, keepdims=True)
    expo = jnp.exp(scores - top)
    total = jnp.sum(expo, axis=0, keepdims=True)
    positive = jnp.sum(jnp.where(hit, scores, 0.0), axis=0, keepdims=True)
    slot = lax.broadcasted_iota(jnp.int32, (8, tile_rows), 0)
    stats[b] = jnp.where(slot == 0, top, jnp.where(slot == 1, total, positive))
    stat_copies = []
    for k in range(1, nb):
        pb, dev = row_peer(k)
        c = remote(stats.at[b], stats.at[b], stats_ss.at[k - 1], stats_rs.at[k - 1], dev)
        c.start()
        stat_copies.append(c)
    for c in stat_copies:
        c.wait_recv()
    every = stats[...]
    row_max = jnp.max(every[:, 0:1, :], axis=0)
    row_sum = jnp.sum(every[:, 1:2, :] * jnp.exp(every[:, 0:1, :] - row_max[None]), axis=0)
    row_pos = jnp.sum(every[:, 2:3, :], axis=0)
    scale = jnp.exp(top - row_max) / row_sum
    weights = (expo * scale - hit.astype(f32)).astype(bf16)

    vid_part = lax.dot_general(weights, captions, (((0,), (0,)), ((), ())), preferred_element_type=f32)
    vid_send[...] = vid_part.astype(bf16).reshape(nb, vrow, width)
    vg_copies = []
    for k in range(1, nb):
        pb, dev = row_peer(k)
        c = remote(vid_send.at[pb], vid_recv.at[k - 1], vg_ss.at[k - 1], vg_rs.at[k - 1], dev)
        c.start()
        vg_copies.append(c)
    cap_part = jnp.dot(weights, videos, preferred_element_type=f32)
    cap_send[...] = cap_part.astype(bf16).reshape(na, ccol, width)
    cg_copies = []
    for k in range(1, na):
        pa, dev = col_peer(k)
        c = remote(cap_send.at[pa], cap_recv.at[k - 1], cg_ss.at[k - 1], cg_rs.at[k - 1], dev)
        c.start()
        cg_copies.append(c)
    loss_v[...] = row_max + jnp.log(row_sum) - row_pos
    loss_ref[...] = loss_v[:, pl.ds(pl.multiple_of(i * rows, rows), rows)]

    vid_grad = vid_send[b].astype(f32)
    for k in range(1, nb):
        vg_copies[k - 1].wait_recv()
        vid_grad = vid_grad + vid_recv[k - 1].astype(f32)
    vid_grad = logit * vid_grad
    vid_dot = jnp.sum(unit_vid * vid_grad, axis=1, keepdims=True)
    raw_all[t] = ((vid_grad - unit_vid * vid_dot) * vid_inv).astype(bf16)
    raw_copies = []
    for k in range(1, tensor):
        pt, dev = tensor_peer(k)
        c = remote(raw_all.at[t], raw_all.at[t], raw_ss.at[k - 1], raw_rs.at[k - 1], dev)
        c.start()
        raw_copies.append(c)

    cap_grad = cap_send[a].astype(f32)
    for k in range(1, na):
        cg_copies[k - 1].wait_recv()
        cap_grad = cap_grad + cap_recv[k - 1].astype(f32)
    cap_grad = logit * cap_grad
    cap_unit = cap_f * cap_inv
    cap_dot = jnp.sum(cap_unit * cap_grad, axis=1, keepdims=True)
    cap_grad_ref[...] = (cap_grad - cap_unit * cap_dot) * cap_inv

    for c in raw_copies:
        c.wait_recv()
    clip_grad_ref[...] = lax.dot_general(
        raw_all[...].reshape(rows, width), proj_v[...], (((1,), (1,)), ((), ())), preferred_element_type=f32
    )
    for group in (part_copies, cap_copies, vid_copies, stat_copies, vg_copies, cg_copies, raw_copies):
        for c in group:
            c.wait_send()


def body(dp, tensor, clip_feats, proj_weight, caption_emb, logit_scale, pair_perm):
    rows, feats = clip_feats.shape
    ccol, width = caption_emb.shape
    inner = inner_size(dp)
    na, nb = dp // inner, inner * tensor
    vrow = rows // tensor
    vmem = pl.BlockSpec(memory_space=pltpu.VMEM)
    anywhere = pl.BlockSpec(memory_space=pl.ANY)
    dma = pltpu.SemaphoreType.DMA
    nr, nc, nt = max(nb - 1, 1), max(na - 1, 1), max(tensor - 1, 1)
    clip_grad, caption_grad, losses = pl.pallas_call(
        functools.partial(kernel, dp, tensor),
        out_shape=(
            jax.ShapeDtypeStruct((rows, feats), f32),
            jax.ShapeDtypeStruct((ccol, width), f32),
            jax.ShapeDtypeStruct((1, rows), f32),
        ),
        in_specs=[pl.BlockSpec(memory_space=pltpu.SMEM), vmem, anywhere, anywhere, anywhere],
        out_specs=(vmem, vmem, vmem),
        scratch_shapes=[
            pltpu.VMEM((rows, feats), bf16),
            pltpu.VMEM(proj_weight.shape, bf16),
            pltpu.VMEM((ccol, width), bf16),
            pltpu.VMEM((tensor, vrow, width), f32),
            pltpu.VMEM((nt, vrow, width), f32),
            pltpu.VMEM((na, ccol, width), bf16),
            pltpu.VMEM((nb, vrow, width), bf16),
            pltpu.VMEM((nb, 8, nb * vrow), f32),
            pltpu.VMEM((1, nb * vrow), f32),
            pltpu.VMEM((nb, vrow, width), bf16),
            pltpu.VMEM((nr, vrow, width), bf16),
            pltpu.VMEM((na, ccol, width), bf16),
            pltpu.VMEM((nc, ccol, width), bf16),
            pltpu.VMEM((tensor, vrow, width), bf16),
            dma((3,)),
            dma((nt,)),
            dma((nt,)),
            dma((nc,)),
            dma((nc,)),
            dma((nr,)),
            dma((nr,)),
            dma((nr,)),
            dma((nr,)),
            dma((nr,)),
            dma((nr,)),
            dma((nc,)),
            dma((nc,)),
            dma((nt,)),
            dma((nt,)),
        ],
        compiler_params=pltpu.CompilerParams(
            collective_id=0, has_side_effects=True, vmem_limit_bytes=48 * 1024 * 1024
        ),
        name="contrastive_step",
    )(logit_scale, pair_perm.reshape(1, -1), clip_feats, proj_weight, caption_emb)
    return clip_grad, caption_grad, losses.reshape(rows)


def solution(mesh):
    return jax.shard_map(
        functools.partial(body, mesh.shape["dp"], mesh.shape["tensor"]),
        mesh=mesh,
        in_specs=(P("dp", "tensor"), P("tensor", None), P(("dp", "tensor"), None), P(), P()),
        out_specs=(P("dp", "tensor"), P(("dp", "tensor"), None), P("dp")),
        check_vma=False,
    )
```

```python
import functools

import jax
import jax.numpy as jnp
from jax import lax
from jax.experimental import pallas as pl
from jax.experimental.pallas import tpu as pltpu
from jax.sharding import PartitionSpec as P

norm_eps = 1e-06
MESH = pl.DeviceIdType.MESH
f32 = jnp.float32
bf16 = jnp.bfloat16


def split(dp):
    pair = 2 if dp % 2 == 0 else 1
    rest = dp // pair
    inner = max(n for n in range(1, rest + 1) if rest % n == 0 and n * n <= rest)
    return rest // inner, inner, pair


def kernel(
    dp,
    tensor,
    logit_ref,
    perm_hbm,
    clip_hbm,
    proj_hbm,
    cap_hbm,
    clip_grad_ref,
    cap_grad_ref,
    loss_ref,
    perm_v,
    clip_v,
    proj_v,
    cap_v,
    part_send,
    part_recv,
    caps,
    vids,
    stats,
    loss_v,
    weights_v,
    cap_acc,
    vid_send,
    vid_recv,
    pre_send,
    pre_recv,
    cap_send,
    cap_recv,
    raw_all,
    load_sem,
    part_ss,
    part_rs,
    caps_ss,
    caps_rs,
    fwd_ss,
    fwd_rs,
    vids_ss,
    vids_rs,
    stats_ss,
    stats_rs,
    vg_ss,
    vg_rs,
    pre_ss,
    pre_rs,
    cg_ss,
    cg_rs,
    raw_ss,
    raw_rs,
):
    outer, inner, pair = split(dp)
    nb = inner * tensor
    rows, feats = clip_v.shape
    vrow = rows // tensor
    ccol, width = cap_v.shape
    tile_cols = outer * pair * ccol
    tile_rows = nb * vrow
    d = lax.axis_index("dp")
    t = lax.axis_index("tensor")
    c = lax.rem(d, pair)
    i = lax.rem(lax.div(d, pair), inner)
    z = lax.div(d, pair * inner)
    b = i * tensor + t

    def dp_index(zz, ii, cc):
        return (zz * inner + ii) * pair + cc

    def row_peer(k):
        pb = lax.rem(b + k, nb)
        return pb, (dp_index(z, lax.div(pb, tensor), c), lax.rem(pb, tensor))

    def col_peer(k):
        pz = lax.rem(z + k, outer)
        return pz, (dp_index(pz, i, c), t)

    def core_peer():
        return (dp_index(z, i, pair - 1 - c), t)

    def tensor_peer(k):
        pt = lax.rem(t + k, tensor)
        return pt, (d, pt)

    started = []

    def send(src, dst, ss, rs, device):
        copy = pltpu.make_async_remote_copy(
            src_ref=src, dst_ref=dst, send_sem=ss, recv_sem=rs, device_id=device, device_id_type=MESH
        )
        copy.start()
        started.append(copy)
        return copy

    loads = [
        pltpu.make_async_copy(src, dst, load_sem.at[n])
        for n, (src, dst) in enumerate(((proj_hbm, proj_v), (clip_hbm, clip_v), (cap_hbm, cap_v), (perm_hbm, perm_v)))
    ]
    for load in loads:
        load.start()
    barrier = pltpu.get_barrier_semaphore()
    peers = [row_peer(k)[1] for k in range(1, nb)] + [col_peer(k)[1] for k in range(1, outer)]
    if pair > 1:
        peers.append(core_peer())
    for device in peers:
        pl.semaphore_signal(barrier, inc=1, device_id=device, device_id_type=MESH)
    logit = logit_ref[0]

    loads[0].wait()
    loads[1].wait()
    part_send[...] = jnp.dot(clip_v[...], proj_v[...], preferred_element_type=f32).reshape(tensor, vrow, width)
    loads[2].wait()
    loads[3].wait()
    cap_f = cap_v[...].astype(f32)
    cap_inv = lax.rsqrt(jnp.sum(cap_f * cap_f, axis=1, keepdims=True) + norm_eps)
    caps[c, z] = (cap_f * cap_inv).astype(bf16)
    pl.semaphore_wait(barrier, len(peers))
    part_copies = []
    for k in range(1, tensor):
        pt, dev = tensor_peer(k)
        part_copies.append(send(part_send.at[pt], part_recv.at[k - 1], part_ss.at[k - 1], part_rs.at[k - 1], dev))
    cap_copies = []
    for k in range(1, outer):
        pz, dev = col_peer(k)
        cap_copies.append(send(caps.at[c, z], caps.at[c, z], caps_ss.at[k - 1], caps_rs.at[k - 1], dev))
    fwd_copies = []
    if pair > 1:
        fwd_copies.append(send(caps.at[c, z], caps.at[c, z], fwd_ss.at[0], fwd_rs.at[0], core_peer()))

    raw_proj = part_send[t]
    for k in range(1, tensor):
        part_copies[k - 1].wait_recv()
        raw_proj = raw_proj + part_recv[k - 1]
    vid_inv = lax.rsqrt(jnp.sum(raw_proj * raw_proj, axis=1, keepdims=True) + norm_eps)
    unit_vid = raw_proj * vid_inv
    vids[b] = unit_vid.astype(bf16)
    vid_copies = []
    for k in range(1, nb):
        pb, dev = row_peer(k)
        vid_copies.append(send(vids.at[b], vids.at[b], vids_ss.at[k - 1], vids_rs.at[k - 1], dev))
    for k in range(1, outer):
        cap_copies[k - 1].wait_recv()
        if pair > 1:
            pz = lax.rem(z + (outer - k), outer)
            fwd_copies.append(send(caps.at[c, pz], caps.at[c, pz], fwd_ss.at[k], fwd_rs.at[k], core_peer()))
    for copy in fwd_copies:
        copy.wait_recv()
    for copy in vid_copies:
        copy.wait_recv()

    captions = caps[...].reshape(tile_cols, width)
    videos = vids[...].reshape(tile_rows, width)
    scores = logit * lax.dot_general(captions, videos, (((1,), (1,)), ((), ())), preferred_element_type=f32)
    wanted = jnp.concatenate(
        [perm_v[:, pl.ds(pl.multiple_of(dp_index(z, n, c) * rows, rows), rows)] for n in range(inner)], axis=1
    )
    index = lax.broadcasted_iota(jnp.int32, (tile_cols, 1), 0)
    block = index // ccol
    column = (dp_index(block % outer, i, block // outer) * tensor + t) * ccol + index % ccol
    hit = column == wanted
    top = jnp.max(scores, axis=0, keepdims=True)
    expo = jnp.exp(scores - top)
    total = jnp.sum(expo, axis=0, keepdims=True)
    positive = jnp.sum(jnp.where(hit, scores, 0.0), axis=0, keepdims=True)
    stats[b] = jnp.concatenate([top, total, positive], axis=1)
    stat_copies = []
    for k in range(1, nb):
        pb, dev = row_peer(k)
        stat_copies.append(send(stats.at[b], stats.at[b], stats_ss.at[k - 1], stats_rs.at[k - 1], dev))
    for copy in stat_copies:
        copy.wait_recv()
    every = [stats[n] for n in range(nb)]
    tops = [v[:, :tile_rows] for v in every]
    row_max = functools.reduce(jnp.maximum, tops)
    row_sum = functools.reduce(
        jnp.add, [v[:, tile_rows : 2 * tile_rows] * jnp.exp(m - row_max) for v, m in zip(every, tops)]
    )
    row_pos = functools.reduce(jnp.add, [v[:, 2 * tile_rows :] for v in every])
    scale = jnp.exp(top - row_max) / row_sum
    weights = (expo * scale - hit.astype(f32)).astype(bf16)
    weights_v[...] = weights.reshape(pair, outer * ccol, tile_rows)

    pre_copies = []
    if pair > 1:
        part = jnp.dot(weights_v[pair - 1 - c], videos, preferred_element_type=f32)
        pre_send[...] = part.astype(bf16).reshape(outer, ccol, width)
        for k in range(outer):
            pz = lax.rem(z + k + 1, outer)
            pre_copies.append(send(pre_send.at[pz], pre_recv.at[k], pre_ss.at[k], pre_rs.at[k], core_peer()))
    vid_part = lax.dot_general(weights, captions, (((0,), (0,)), ((), ())), preferred_element_type=f32)
    vid_send[...] = vid_part.astype(bf16).reshape(nb, vrow, width)
    vg_copies = []
    for k in range(1, nb):
        pb, dev = row_peer(k)
        vg_copies.append(send(vid_send.at[pb], vid_recv.at[k - 1], vg_ss.at[k - 1], vg_rs.at[k - 1], dev))
    own = jnp.dot(weights_v[c], videos, preferred_element_type=f32)
    cap_acc[...] = own.reshape(outer, ccol, width)
    cg_copies = []
    for k in range(outer):
        pz = lax.rem(z + k + 1, outer)
        block_sum = cap_acc[pz]
        if pair > 1:
            pre_copies[k].wait_recv()
            block_sum = block_sum + pre_recv[k].astype(f32)
        if k < outer - 1:
            cap_send[k] = block_sum.astype(bf16)
            cg_copies.append(send(cap_send.at[k], cap_recv.at[k], cg_ss.at[k], cg_rs.at[k], col_peer(k + 1)[1]))
    cap_grad = block_sum
    loss_v[...] = row_max + jnp.log(row_sum) - row_pos
    loss_ref[...] = loss_v[:, pl.ds(pl.multiple_of(i * rows, rows), rows)]

    vid_grad = vid_send[b].astype(f32)
    for k in range(1, nb):
        vg_copies[k - 1].wait_recv()
        vid_grad = vid_grad + vid_recv[k - 1].astype(f32)
    vid_grad = logit * vid_grad
    vid_dot = jnp.sum(unit_vid * vid_grad, axis=1, keepdims=True)
    raw_all[t] = ((vid_grad - unit_vid * vid_dot) * vid_inv).astype(bf16)
    raw_copies = []
    for k in range(1, tensor):
        pt, dev = tensor_peer(k)
        raw_copies.append(send(raw_all.at[t], raw_all.at[t], raw_ss.at[k - 1], raw_rs.at[k - 1], dev))

    for k in range(outer - 1):
        cg_copies[k].wait_recv()
        cap_grad = cap_grad + cap_recv[k].astype(f32)
    cap_grad = logit * cap_grad
    cap_unit = cap_f * cap_inv
    cap_dot = jnp.sum(cap_unit * cap_grad, axis=1, keepdims=True)
    cap_grad_ref[...] = (cap_grad - cap_unit * cap_dot) * cap_inv

    for copy in raw_copies:
        copy.wait_recv()
    clip_grad_ref[...] = lax.dot_general(
        raw_all[...].reshape(rows, width), proj_v[...], (((1,), (1,)), ((), ())), preferred_element_type=f32
    )
    for copy in started:
        copy.wait_send()


def body(dp, tensor, clip_feats, proj_weight, caption_emb, logit_scale, pair_perm):
    rows, feats = clip_feats.shape
    ccol, width = caption_emb.shape
    outer, inner, pair = split(dp)
    nb = inner * tensor
    vrow = rows // tensor
    tile_rows = nb * vrow
    vmem = pl.BlockSpec(memory_space=pltpu.VMEM)
    hbm = pl.BlockSpec(memory_space=pltpu.HBM)
    dma = pltpu.SemaphoreType.DMA
    nr, no, nt = max(nb - 1, 1), max(outer - 1, 1), max(tensor - 1, 1)
    clip_grad, caption_grad, losses = pl.pallas_call(
        functools.partial(kernel, dp, tensor),
        out_shape=(
            jax.ShapeDtypeStruct((rows, feats), f32),
            jax.ShapeDtypeStruct((ccol, width), f32),
            jax.ShapeDtypeStruct((1, rows), f32),
        ),
        in_specs=[pl.BlockSpec(memory_space=pltpu.SMEM), hbm, hbm, hbm, hbm],
        out_specs=(vmem, vmem, vmem),
        scratch_shapes=[
            pltpu.VMEM((1, pair_perm.shape[0]), jnp.int32),
            pltpu.VMEM((rows, feats), bf16),
            pltpu.VMEM(proj_weight.shape, bf16),
            pltpu.VMEM((ccol, width), bf16),
            pltpu.VMEM((tensor, vrow, width), f32),
            pltpu.VMEM((nt, vrow, width), f32),
            pltpu.VMEM((pair, outer, ccol, width), bf16),
            pltpu.VMEM((nb, vrow, width), bf16),
            pltpu.VMEM((nb, 1, 3 * tile_rows), f32),
            pltpu.VMEM((1, tile_rows), f32),
            pltpu.VMEM((pair, outer * ccol, tile_rows), bf16),
            pltpu.VMEM((outer, ccol, width), f32),
            pltpu.VMEM((nb, vrow, width), bf16),
            pltpu.VMEM((nr, vrow, width), bf16),
            pltpu.VMEM((outer, ccol, width), bf16),
            pltpu.VMEM((outer, ccol, width), bf16),
            pltpu.VMEM((no, ccol, width), bf16),
            pltpu.VMEM((no, ccol, width), bf16),
            pltpu.VMEM((tensor, vrow, width), bf16),
            dma((4,)),
            *[dma((nt,))] * 2,
            *[dma((no,))] * 2,
            *[dma((outer,))] * 2,
            *[dma((nr,))] * 2,
            *[dma((nr,))] * 2,
            *[dma((nr,))] * 2,
            *[dma((outer,))] * 2,
            *[dma((no,))] * 2,
            *[dma((nt,))] * 2,
        ],
        compiler_params=pltpu.CompilerParams(collective_id=0, has_side_effects=True, vmem_limit_bytes=67043328),
        name="contrastive_step",
    )(logit_scale, pair_perm.reshape(1, -1), clip_feats, proj_weight, caption_emb)
    return clip_grad, caption_grad, losses.reshape(rows)


def solution(mesh):
    return jax.shard_map(
        functools.partial(body, mesh.shape["dp"], mesh.shape["tensor"]),
        mesh=mesh,
        in_specs=(P("dp", "tensor"), P("tensor", None), P(("dp", "tensor"), None), P(), P()),
        out_specs=(P("dp", "tensor"), P(("dp", "tensor"), None), P("dp")),
        check_vma=False,
    )
```

```python
import functools

import jax
import jax.numpy as jnp
from jax import lax
from jax.experimental import pallas as pl
from jax.experimental.pallas import tpu as pltpu
from jax.sharding import PartitionSpec as P

norm_eps = 1e-06
MESH = pl.DeviceIdType.MESH
f32 = jnp.float32
bf16 = jnp.bfloat16


def split(dp):
    pair = 2 if dp % 2 == 0 else 1
    rest = dp // pair
    inner = max(n for n in range(1, rest + 1) if rest % n == 0 and n * n <= rest)
    return rest // inner, inner, pair


def kernel(
    dp,
    tensor,
    logit_ref,
    perm_hbm,
    clip_hbm,
    proj_hbm,
    cap_hbm,
    clip_grad_ref,
    cap_grad_ref,
    loss_ref,
    perm_v,
    clip_v,
    proj_v,
    cap_v,
    part_send,
    part_recv,
    caps,
    vids,
    stats,
    loss_v,
    weights_v,
    cap_acc,
    vid_send,
    vid_recv,
    pre_send,
    pre_recv,
    cap_send,
    cap_recv,
    raw_all,
    load_sem,
    part_ss,
    part_rs,
    caps_ss,
    caps_rs,
    fwd_ss,
    fwd_rs,
    vids_ss,
    vids_rs,
    stats_ss,
    stats_rs,
    vg_ss,
    vg_rs,
    pre_ss,
    pre_rs,
    cg_ss,
    cg_rs,
    raw_ss,
    raw_rs,
):
    outer, inner, pair = split(dp)
    nb = inner * tensor
    rows, feats = clip_v.shape
    vrow = rows // tensor
    ccol, width = cap_v.shape
    tile_cols = outer * pair * ccol
    tile_rows = nb * vrow
    d = lax.axis_index("dp")
    t = lax.axis_index("tensor")
    c = lax.rem(d, pair)
    i = lax.rem(lax.div(d, pair), inner)
    z = lax.div(d, pair * inner)
    b = i * tensor + t

    def dp_index(zz, ii, cc):
        return (zz * inner + ii) * pair + cc

    def row_peer(k):
        pb = lax.rem(b + k, nb)
        return pb, (dp_index(z, lax.div(pb, tensor), c), lax.rem(pb, tensor))

    def col_peer(k):
        pz = lax.rem(z + k, outer)
        return pz, (dp_index(pz, i, c), t)

    def core_peer():
        return (dp_index(z, i, pair - 1 - c), t)

    def tensor_peer(k):
        pt = lax.rem(t + k, tensor)
        return pt, (d, pt)

    started = []

    def send(src, dst, ss, rs, device):
        copy = pltpu.make_async_remote_copy(
            src_ref=src, dst_ref=dst, send_sem=ss, recv_sem=rs, device_id=device, device_id_type=MESH
        )
        copy.start()
        started.append(copy)
        return copy

    loads = [
        pltpu.make_async_copy(src, dst, load_sem.at[n])
        for n, (src, dst) in enumerate(((proj_hbm, proj_v), (clip_hbm, clip_v), (cap_hbm, cap_v), (perm_hbm, perm_v)))
    ]
    for load in loads:
        load.start()
    barrier = pltpu.get_barrier_semaphore()
    peers = [row_peer(k)[1] for k in range(1, nb)] + [col_peer(k)[1] for k in range(1, outer)]
    if pair > 1:
        peers.append(core_peer())
    for device in peers:
        pl.semaphore_signal(barrier, inc=1, device_id=device, device_id_type=MESH)
    logit = logit_ref[0]

    loads[0].wait()
    loads[1].wait()
    part_send[...] = jnp.dot(clip_v[...], proj_v[...], preferred_element_type=f32).reshape(tensor, vrow, width)
    loads[2].wait()
    loads[3].wait()
    cap_f = cap_v[...].astype(f32)
    cap_inv = lax.rsqrt(jnp.sum(cap_f * cap_f, axis=1, keepdims=True) + norm_eps)
    caps[c, z] = (cap_f * cap_inv).astype(bf16)
    pl.semaphore_wait(barrier, len(peers))
    part_copies = []
    for k in range(1, tensor):
        pt, dev = tensor_peer(k)
        part_copies.append(send(part_send.at[pt], part_recv.at[k - 1], part_ss.at[k - 1], part_rs.at[k - 1], dev))
    cap_copies = []
    for k in range(1, outer):
        pz, dev = col_peer(k)
        cap_copies.append(send(caps.at[c, z], caps.at[c, z], caps_ss.at[k - 1], caps_rs.at[k - 1], dev))
    fwd_copies = []
    if pair > 1:
        fwd_copies.append(send(caps.at[c, z], caps.at[c, z], fwd_ss.at[0], fwd_rs.at[0], core_peer()))

    raw_proj = part_send[t]
    for k in range(1, tensor):
        part_copies[k - 1].wait_recv()
        raw_proj = raw_proj + part_recv[k - 1]
    vid_inv = lax.rsqrt(jnp.sum(raw_proj * raw_proj, axis=1, keepdims=True) + norm_eps)
    unit_vid = raw_proj * vid_inv
    vids[b] = unit_vid.astype(bf16)
    vid_copies = []
    for k in range(1, nb):
        pb, dev = row_peer(k)
        vid_copies.append(send(vids.at[b], vids.at[b], vids_ss.at[k - 1], vids_rs.at[k - 1], dev))
    for k in range(1, outer):
        cap_copies[k - 1].wait_recv()
        if pair > 1:
            pz = lax.rem(z + (outer - k), outer)
            fwd_copies.append(send(caps.at[c, pz], caps.at[c, pz], fwd_ss.at[k], fwd_rs.at[k], core_peer()))
    for copy in fwd_copies:
        copy.wait_recv()
    for copy in vid_copies:
        copy.wait_recv()

    captions = caps[...].reshape(tile_cols, width)
    videos = vids[...].reshape(tile_rows, width)
    scores = logit * lax.dot_general(captions, videos, (((1,), (1,)), ((), ())), preferred_element_type=f32)
    wanted = jnp.concatenate(
        [perm_v[:, pl.ds(pl.multiple_of(dp_index(z, n, c) * rows, rows), rows)] for n in range(inner)], axis=1
    )
    index = lax.broadcasted_iota(jnp.int32, (tile_cols, 1), 0)
    block = index // ccol
    column = (dp_index(block % outer, i, block // outer) * tensor + t) * ccol + index % ccol
    hit = column == wanted
    top = jnp.max(scores, axis=0, keepdims=True)
    expo = jnp.exp(scores - top)
    total = jnp.sum(expo, axis=0, keepdims=True)
    positive = jnp.sum(jnp.where(hit, scores, 0.0), axis=0, keepdims=True)
    stats[b] = jnp.concatenate([top, total, positive], axis=1)
    stat_copies = []
    for k in range(1, nb):
        pb, dev = row_peer(k)
        stat_copies.append(send(stats.at[b], stats.at[b], stats_ss.at[k - 1], stats_rs.at[k - 1], dev))
    for copy in stat_copies:
        copy.wait_recv()
    every = [stats[n] for n in range(nb)]
    tops = [v[:, :tile_rows] for v in every]
    row_max = functools.reduce(jnp.maximum, tops)
    row_sum = functools.reduce(
        jnp.add, [v[:, tile_rows : 2 * tile_rows] * jnp.exp(m - row_max) for v, m in zip(every, tops)]
    )
    row_pos = functools.reduce(jnp.add, [v[:, 2 * tile_rows :] for v in every])
    scale = jnp.exp(top - row_max) / row_sum
    weights = (expo * scale - hit.astype(f32)).astype(bf16)
    weights_v[...] = weights.reshape(pair, outer * ccol, tile_rows)

    pre_copies = []
    if pair > 1:
        part = jnp.dot(weights_v[pair - 1 - c], videos, preferred_element_type=f32)
        pre_send[...] = part.astype(bf16).reshape(outer, ccol, width)
        for k in range(outer):
            pz = lax.rem(z + k + 1, outer)
            pre_copies.append(send(pre_send.at[pz], pre_recv.at[k], pre_ss.at[k], pre_rs.at[k], core_peer()))
    vid_part = lax.dot_general(weights, captions, (((0,), (0,)), ((), ())), preferred_element_type=f32)
    vid_send[...] = vid_part.astype(bf16).reshape(nb, vrow, width)
    vg_copies = []
    for k in range(1, nb):
        pb, dev = row_peer(k)
        vg_copies.append(send(vid_send.at[pb], vid_recv.at[k - 1], vg_ss.at[k - 1], vg_rs.at[k - 1], dev))
    own = jnp.dot(weights_v[c], videos, preferred_element_type=f32)
    cap_acc[...] = own.reshape(outer, ccol, width)
    cg_copies = []
    for k in range(outer):
        pz = lax.rem(z + k + 1, outer)
        block_sum = cap_acc[pz]
        if pair > 1:
            pre_copies[k].wait_recv()
            block_sum = block_sum + pre_recv[k].astype(f32)
        if k < outer - 1:
            cap_send[k] = block_sum.astype(bf16)
            cg_copies.append(send(cap_send.at[k], cap_recv.at[k], cg_ss.at[k], cg_rs.at[k], col_peer(k + 1)[1]))
    cap_grad = block_sum
    loss_v[...] = row_max + jnp.log(row_sum) - row_pos
    loss_ref[...] = loss_v[:, pl.ds(pl.multiple_of(i * rows, rows), rows)]

    vid_grad = vid_send[b].astype(f32)
    for k in range(1, nb):
        vg_copies[k - 1].wait_recv()
        vid_grad = vid_grad + vid_recv[k - 1].astype(f32)
    vid_grad = logit * vid_grad
    vid_dot = jnp.sum(unit_vid * vid_grad, axis=1, keepdims=True)
    raw_all[t] = ((vid_grad - unit_vid * vid_dot) * vid_inv).astype(bf16)
    raw_copies = []
    for k in range(1, tensor):
        pt, dev = tensor_peer(k)
        raw_copies.append(send(raw_all.at[t], raw_all.at[t], raw_ss.at[k - 1], raw_rs.at[k - 1], dev))

    for k in range(outer - 1):
        cg_copies[k].wait_recv()
        cap_grad = cap_grad + cap_recv[k].astype(f32)
    cap_grad = logit * cap_grad
    cap_unit = cap_f * cap_inv
    cap_dot = jnp.sum(cap_unit * cap_grad, axis=1, keepdims=True)
    cap_grad_ref[...] = (cap_grad - cap_unit * cap_dot) * cap_inv

    for copy in raw_copies:
        copy.wait_recv()
    clip_grad_ref[...] = lax.dot_general(
        raw_all[...].reshape(rows, width), proj_v[...], (((1,), (1,)), ((), ())), preferred_element_type=f32
    )
    for copy in started:
        copy.wait_send()


def store_kernel(*refs):
    count = len(refs) // 2
    sems = refs[-1]
    copies = [pltpu.make_async_copy(refs[n], refs[count + n], sems.at[n]) for n in range(count)]
    for copy in copies:
        copy.start()
    for copy in copies:
        copy.wait()


def store_results(*values):
    return pl.pallas_call(
        store_kernel,
        out_shape=tuple(jax.ShapeDtypeStruct(v.shape, v.dtype) for v in values),
        in_specs=[pl.BlockSpec(memory_space=pltpu.VMEM)] * len(values),
        out_specs=tuple(pl.BlockSpec(memory_space=pltpu.HBM) for v in values),
        scratch_shapes=[pltpu.SemaphoreType.DMA((len(values),))],
        compiler_params=pltpu.CompilerParams(vmem_limit_bytes=4 * 1024 * 1024),
        name="store_results",
    )(*values)


def body(dp, tensor, clip_feats, proj_weight, caption_emb, logit_scale, pair_perm):
    rows, feats = clip_feats.shape
    ccol, width = caption_emb.shape
    outer, inner, pair = split(dp)
    nb = inner * tensor
    vrow = rows // tensor
    tile_rows = nb * vrow
    vmem = pl.BlockSpec(memory_space=pltpu.VMEM)
    hbm = pl.BlockSpec(memory_space=pltpu.HBM)
    dma = pltpu.SemaphoreType.DMA
    nr, no, nt = max(nb - 1, 1), max(outer - 1, 1), max(tensor - 1, 1)
    clip_grad, caption_grad, losses = pl.pallas_call(
        functools.partial(kernel, dp, tensor),
        out_shape=(
            jax.ShapeDtypeStruct((rows, feats), f32),
            jax.ShapeDtypeStruct((ccol, width), f32),
            jax.ShapeDtypeStruct((1, rows), f32),
        ),
        in_specs=[pl.BlockSpec(memory_space=pltpu.SMEM), hbm, hbm, hbm, hbm],
        out_specs=(vmem, vmem, vmem),
        scratch_shapes=[
            pltpu.VMEM((1, pair_perm.shape[0]), jnp.int32),
            pltpu.VMEM((rows, feats), bf16),
            pltpu.VMEM(proj_weight.shape, bf16),
            pltpu.VMEM((ccol, width), bf16),
            pltpu.VMEM((tensor, vrow, width), f32),
            pltpu.VMEM((nt, vrow, width), f32),
            pltpu.VMEM((pair, outer, ccol, width), bf16),
            pltpu.VMEM((nb, vrow, width), bf16),
            pltpu.VMEM((nb, 1, 3 * tile_rows), f32),
            pltpu.VMEM((1, tile_rows), f32),
            pltpu.VMEM((pair, outer * ccol, tile_rows), bf16),
            pltpu.VMEM((outer, ccol, width), f32),
            pltpu.VMEM((nb, vrow, width), bf16),
            pltpu.VMEM((nr, vrow, width), bf16),
            pltpu.VMEM((outer, ccol, width), bf16),
            pltpu.VMEM((outer, ccol, width), bf16),
            pltpu.VMEM((no, ccol, width), bf16),
            pltpu.VMEM((no, ccol, width), bf16),
            pltpu.VMEM((tensor, vrow, width), bf16),
            dma((4,)),
            *[dma((nt,))] * 2,
            *[dma((no,))] * 2,
            *[dma((outer,))] * 2,
            *[dma((nr,))] * 2,
            *[dma((nr,))] * 2,
            *[dma((nr,))] * 2,
            *[dma((outer,))] * 2,
            *[dma((no,))] * 2,
            *[dma((nt,))] * 2,
        ],
        compiler_params=pltpu.CompilerParams(collective_id=0, has_side_effects=True, vmem_limit_bytes=48 * 1024 * 1024),
        name="contrastive_step",
    )(logit_scale, *[pltpu.with_memory_space_constraint(x, pltpu.HBM) for x in (pair_perm.reshape(1, -1), clip_feats, proj_weight, caption_emb)])
    clip_grad, caption_grad, losses = store_results(clip_grad, caption_grad, losses)
    return clip_grad, caption_grad, losses.reshape(rows)


def solution(mesh):
    return jax.shard_map(
        functools.partial(body, mesh.shape["dp"], mesh.shape["tensor"]),
        mesh=mesh,
        in_specs=(P("dp", "tensor"), P("tensor", None), P(("dp", "tensor"), None), P(), P()),
        out_specs=(P("dp", "tensor"), P(("dp", "tensor"), None), P("dp")),
        check_vma=False,
    )
```

```python
import functools

import jax
import jax.numpy as jnp
from jax import lax
from jax.experimental import pallas as pl
from jax.experimental.pallas import tpu as pltpu
from jax.sharding import PartitionSpec as P

norm_eps = 1e-06
MESH = pl.DeviceIdType.MESH
f32 = jnp.float32
bf16 = jnp.bfloat16


def split(dp):
    pair = 2 if dp % 2 == 0 else 1
    rest = dp // pair
    inner = max(n for n in range(1, rest + 1) if rest % n == 0 and n * n <= rest)
    return rest // inner, inner, pair


def chunks(vrow):
    return max(n for n in (1, 2, 2) if vrow % (16 * n) == 0 or n == 1)


def kernel(
    dp,
    tensor,
    logit_ref,
    perm_hbm,
    clip_hbm,
    proj_hbm,
    cap_hbm,
    clip_grad_ref,
    cap_grad_ref,
    loss_ref,
    perm_v,
    clip_v,
    proj_v,
    cap_v,
    part_send,
    part_recv,
    caps,
    vids,
    stats,
    loss_v,
    weights_v,
    cap_acc,
    vid_send,
    vid_recv,
    pre_send,
    pre_recv,
    cap_send,
    cap_recv,
    raw_all,
    load_sem,
    part_ss,
    part_rs,
    caps_ss,
    caps_rs,
    fwd_ss,
    fwd_rs,
    vids_ss,
    vids_rs,
    stats_ss,
    stats_rs,
    vg_ss,
    vg_rs,
    pre_ss,
    pre_rs,
    cg_ss,
    cg_rs,
    raw_ss,
    raw_rs,
):
    outer, inner, pair = split(dp)
    nb = inner * tensor
    rows, feats = clip_v.shape
    vrow = rows // tensor
    ccol, width = cap_v.shape
    tile_cols = outer * pair * ccol
    nq = chunks(vrow)
    pieces = [pl.ds(q * (vrow // nq), vrow // nq) for q in range(nq)]
    tile_rows = nb * vrow
    d = lax.axis_index("dp")
    t = lax.axis_index("tensor")
    c = lax.rem(d, pair)
    i = lax.rem(lax.div(d, pair), inner)
    z = lax.div(d, pair * inner)
    b = i * tensor + t

    def dp_index(zz, ii, cc):
        return (zz * inner + ii) * pair + cc

    def row_peer(k):
        pb = lax.rem(b + k, nb)
        return pb, (dp_index(z, lax.div(pb, tensor), c), lax.rem(pb, tensor))

    def col_peer(k):
        pz = lax.rem(z + k, outer)
        return pz, (dp_index(pz, i, c), t)

    def core_peer():
        return (dp_index(z, i, pair - 1 - c), t)

    def tensor_peer(k):
        pt = lax.rem(t + k, tensor)
        return pt, (d, pt)

    started = []

    def send(src, dst, ss, rs, device):
        copy = pltpu.make_async_remote_copy(
            src_ref=src, dst_ref=dst, send_sem=ss, recv_sem=rs, device_id=device, device_id_type=MESH
        )
        copy.start()
        started.append(copy)
        return copy

    loads = [
        pltpu.make_async_copy(src, dst, load_sem.at[n])
        for n, (src, dst) in enumerate(((proj_hbm, proj_v), (clip_hbm, clip_v), (cap_hbm, cap_v), (perm_hbm, perm_v)))
    ]
    for load in loads:
        load.start()
    barrier = pltpu.get_barrier_semaphore()
    peers = [row_peer(k)[1] for k in range(1, nb)] + [col_peer(k)[1] for k in range(1, outer)]
    if pair > 1:
        peers.append(core_peer())
    for device in peers:
        pl.semaphore_signal(barrier, inc=1, device_id=device, device_id_type=MESH)

    loads[0].wait()
    loads[1].wait()
    part_send[...] = jnp.dot(clip_v[...], proj_v[...], preferred_element_type=f32).reshape(tensor, vrow, width)
    loads[2].wait()
    loads[3].wait()
    logit = logit_ref[0]
    cap_f = cap_v[...].astype(f32)
    cap_inv = lax.rsqrt(jnp.sum(cap_f * cap_f, axis=1, keepdims=True) + norm_eps)
    caps[c, z] = (cap_f * cap_inv).astype(bf16)
    pl.semaphore_wait(barrier, len(peers))
    part_copies = []
    for q, piece in enumerate(pieces):
        for k in range(1, tensor):
            pt, dev = tensor_peer(k)
            src, dst = part_send.at[pt, piece], part_recv.at[k - 1, piece]
            part_copies.append(send(src, dst, part_ss.at[k - 1, q], part_rs.at[k - 1, q], dev))
    cap_copies = []
    for k in range(1, outer):
        pz, dev = col_peer(k)
        cap_copies.append(send(caps.at[c, z], caps.at[c, z], caps_ss.at[k - 1], caps_rs.at[k - 1], dev))
    fwd_copies = []
    if pair > 1:
        fwd_copies.append(send(caps.at[c, z], caps.at[c, z], fwd_ss.at[0], fwd_rs.at[0], core_peer()))

    unit_vid, vid_inv, vid_copies = [], [], []
    for q, piece in enumerate(pieces):
        raw_proj = part_send[t, piece]
        for k in range(1, tensor):
            part_copies[q * (tensor - 1) + k - 1].wait_recv()
            raw_proj = raw_proj + part_recv[k - 1, piece]
        inverse = lax.rsqrt(jnp.sum(raw_proj * raw_proj, axis=1, keepdims=True) + norm_eps)
        vid_inv.append(inverse)
        unit_vid.append(raw_proj * inverse)
        vids[b, piece] = unit_vid[q].astype(bf16)
        for k in range(1, nb):
            pb, dev = row_peer(k)
            here = vids.at[b, piece]
            vid_copies.append(send(here, here, vids_ss.at[k - 1, q], vids_rs.at[k - 1, q], dev))
    for k in range(outer - 1, 0, -1):
        cap_copies[k - 1].wait_recv()
        if pair > 1:
            pz = lax.rem(z + (outer - k), outer)
            fwd_copies.append(send(caps.at[c, pz], caps.at[c, pz], fwd_ss.at[k], fwd_rs.at[k], core_peer()))
    for copy in fwd_copies:
        copy.wait_recv()
    for copy in vid_copies:
        copy.wait_recv()

    captions = caps[...].reshape(tile_cols, width)
    videos = vids[...].reshape(tile_rows, width)
    scores = logit * lax.dot_general(captions, videos, (((1,), (1,)), ((), ())), preferred_element_type=f32)
    wanted = jnp.concatenate(
        [perm_v[:, pl.ds(pl.multiple_of(dp_index(z, n, c) * rows, rows), rows)] for n in range(inner)], axis=1
    )
    index = lax.broadcasted_iota(jnp.int32, (tile_cols, 1), 0)
    block = index // ccol
    column = (dp_index(block % outer, i, block // outer) * tensor + t) * ccol + index % ccol
    hit = column == wanted
    top = jnp.max(scores, axis=0, keepdims=True)
    expo = jnp.exp(scores - top)
    total = jnp.sum(expo, axis=0, keepdims=True)
    positive = jnp.sum(jnp.where(hit, scores, 0.0), axis=0, keepdims=True)
    stats[b] = jnp.concatenate([top, total, positive], axis=1)
    stat_copies = []
    for k in range(1, nb):
        pb, dev = row_peer(k)
        stat_copies.append(send(stats.at[b], stats.at[b], stats_ss.at[k - 1], stats_rs.at[k - 1], dev))
    for copy in stat_copies:
        copy.wait_recv()
    every = [stats[n] for n in range(nb)]
    tops = [v[:, :tile_rows] for v in every]
    row_max = functools.reduce(jnp.maximum, tops)
    row_sum = functools.reduce(
        jnp.add, [v[:, tile_rows : 2 * tile_rows] * jnp.exp(m - row_max) for v, m in zip(every, tops)]
    )
    row_pos = functools.reduce(jnp.add, [v[:, 2 * tile_rows :] for v in every])
    scale = jnp.exp(top - row_max) / row_sum
    weights = (expo * scale - hit.astype(f32)).astype(bf16)
    weights_v[...] = weights.reshape(pair, outer * ccol, tile_rows)

    vid_part = lax.dot_general(weights, captions, (((0,), (0,)), ((), ())), preferred_element_type=f32)
    vid_send[...] = vid_part.astype(bf16).reshape(nb, vrow, width)
    vg_copies = []
    for q, piece in enumerate(pieces):
        for k in range(1, nb):
            pb, dev = row_peer(k)
            src, dst = vid_send.at[pb, piece], vid_recv.at[k - 1, piece]
            vg_copies.append(send(src, dst, vg_ss.at[k - 1, q], vg_rs.at[k - 1, q], dev))
    pre_copies = []
    if pair > 1:
        part = jnp.dot(weights_v[pair - 1 - c], videos, preferred_element_type=f32)
        pre_send[...] = part.astype(bf16).reshape(outer, ccol, width)
        for k in range(outer):
            pz = lax.rem(z + k + 1, outer)
            pre_copies.append(send(pre_send.at[pz], pre_recv.at[k], pre_ss.at[k], pre_rs.at[k], core_peer()))
    own = jnp.dot(weights_v[c], videos, preferred_element_type=f32)
    cap_acc[...] = own.reshape(outer, ccol, width)
    cg_copies = []
    for k in range(outer):
        pz = lax.rem(z + k + 1, outer)
        block_sum = cap_acc[pz]
        if pair > 1:
            pre_copies[k].wait_recv()
            block_sum = block_sum + pre_recv[k].astype(f32)
        if k < outer - 1:
            cap_send[k] = block_sum.astype(bf16)
            cg_copies.append(send(cap_send.at[k], cap_recv.at[k], cg_ss.at[k], cg_rs.at[k], col_peer(k + 1)[1]))
    cap_grad = block_sum
    raw_copies = []
    for q, piece in enumerate(pieces):
        vid_grad = vid_send[b, piece].astype(f32)
        for k in range(1, nb):
            vg_copies[q * (nb - 1) + k - 1].wait_recv()
            vid_grad = vid_grad + vid_recv[k - 1, piece].astype(f32)
        vid_grad = logit * vid_grad
        vid_dot = jnp.sum(unit_vid[q] * vid_grad, axis=1, keepdims=True)
        raw_all[t, piece] = ((vid_grad - unit_vid[q] * vid_dot) * vid_inv[q]).astype(bf16)
        for k in range(1, tensor):
            pt, dev = tensor_peer(k)
            here = raw_all.at[t, piece]
            raw_copies.append(send(here, here, raw_ss.at[k - 1, q], raw_rs.at[k - 1, q], dev))

    def clip_rows(owner):
        clip_grad_ref[pl.ds(pl.multiple_of(owner * vrow, vrow), vrow), :] = lax.dot_general(
            raw_all[owner], proj_v[...], (((1,), (1,)), ((), ())), preferred_element_type=f32
        )

    clip_rows(t)
    loss_v[...] = row_max + jnp.log(row_sum) - row_pos
    loss_ref[...] = loss_v[:, pl.ds(pl.multiple_of(i * rows, rows), rows)]
    for k in range(outer - 1):
        cg_copies[k].wait_recv()
        cap_grad = cap_grad + cap_recv[k].astype(f32)
    cap_grad = logit * cap_grad
    cap_unit = cap_f * cap_inv
    cap_dot = jnp.sum(cap_unit * cap_grad, axis=1, keepdims=True)
    cap_grad_ref[...] = (cap_grad - cap_unit * cap_dot) * cap_inv

    for k in range(1, tensor):
        for q in range(nq):
            raw_copies[q * (tensor - 1) + k - 1].wait_recv()
        clip_rows(lax.rem(t + (tensor - k), tensor))
    for copy in started:
        copy.wait_send()


def store_kernel(*refs):
    count = len(refs) // 2
    sems = refs[-1]
    copies = [pltpu.make_async_copy(refs[n], refs[count + n], sems.at[n]) for n in range(count)]
    for copy in copies:
        copy.start()
    for copy in copies:
        copy.wait()


def store_results(*values):
    return pl.pallas_call(
        store_kernel,
        out_shape=tuple(jax.ShapeDtypeStruct(v.shape, v.dtype) for v in values),
        in_specs=[pl.BlockSpec(memory_space=pltpu.VMEM)] * len(values),
        out_specs=tuple(pl.BlockSpec(memory_space=pltpu.HBM) for v in values),
        scratch_shapes=[pltpu.SemaphoreType.DMA((len(values),))],
        compiler_params=pltpu.CompilerParams(vmem_limit_bytes=4 * 1024 * 1024),
        name="store_results",
    )(*values)


def body(dp, tensor, clip_feats, proj_weight, caption_emb, logit_scale, pair_perm):
    rows, feats = clip_feats.shape
    ccol, width = caption_emb.shape
    outer, inner, pair = split(dp)
    nb = inner * tensor
    vrow = rows // tensor
    tile_rows = nb * vrow
    nq = chunks(vrow)
    vmem = pl.BlockSpec(memory_space=pltpu.VMEM)
    hbm = pl.BlockSpec(memory_space=pltpu.HBM)
    dma = pltpu.SemaphoreType.DMA
    nr, no, nt = max(nb - 1, 1), max(outer - 1, 1), max(tensor - 1, 1)
    clip_grad, caption_grad, losses = pl.pallas_call(
        functools.partial(kernel, dp, tensor),
        out_shape=(
            jax.ShapeDtypeStruct((rows, feats), f32),
            jax.ShapeDtypeStruct((ccol, width), f32),
            jax.ShapeDtypeStruct((1, rows), f32),
        ),
        in_specs=[pl.BlockSpec(memory_space=pltpu.SMEM)] + [hbm] * 4,
        out_specs=(vmem, vmem, vmem),
        scratch_shapes=[
            pltpu.VMEM((1, pair_perm.shape[0]), jnp.int32),
            pltpu.VMEM((rows, feats), bf16),
            pltpu.VMEM(proj_weight.shape, bf16),
            pltpu.VMEM((ccol, width), bf16),
            pltpu.VMEM((tensor, vrow, width), f32),
            pltpu.VMEM((nt, vrow, width), f32),
            pltpu.VMEM((pair, outer, ccol, width), bf16),
            pltpu.VMEM((nb, vrow, width), bf16),
            pltpu.VMEM((nb, 1, 3 * tile_rows), f32),
            pltpu.VMEM((1, tile_rows), f32),
            pltpu.VMEM((pair, outer * ccol, tile_rows), bf16),
            pltpu.VMEM((outer, ccol, width), f32),
            pltpu.VMEM((nb, vrow, width), bf16),
            pltpu.VMEM((nr, vrow, width), bf16),
            pltpu.VMEM((outer, ccol, width), bf16),
            pltpu.VMEM((outer, ccol, width), bf16),
            pltpu.VMEM((no, ccol, width), bf16),
            pltpu.VMEM((no, ccol, width), bf16),
            pltpu.VMEM((tensor, vrow, width), bf16),
            dma((4,)),
            *[dma((nt, nq))] * 2,
            *[dma((no,))] * 2,
            *[dma((outer,))] * 2,
            *[dma((nr, nq))] * 2,
            *[dma((nr,))] * 2,
            *[dma((nr, nq))] * 2,
            *[dma((outer,))] * 2,
            *[dma((no,))] * 2,
            *[dma((nt, nq))] * 2,
        ],
        compiler_params=pltpu.CompilerParams(collective_id=0, has_side_effects=True, vmem_limit_bytes=48 * 1024 * 1024),
        name="contrastive_step",
    )(
        logit_scale,
        *[
            pltpu.with_memory_space_constraint(x, pltpu.HBM)
            for x in (pair_perm.reshape(1, -1), clip_feats, proj_weight, caption_emb)
        ]
    )
    clip_grad, caption_grad, losses = store_results(clip_grad, caption_grad, losses)
    return clip_grad, caption_grad, losses.reshape(rows)


def solution(mesh):
    return jax.shard_map(
        functools.partial(body, mesh.shape["dp"], mesh.shape["tensor"]),
        mesh=mesh,
        in_specs=(P("dp", "tensor"), P("tensor", None), P(("dp", "tensor"), None), P(), P()),
        out_specs=(P("dp", "tensor"), P(("dp", "tensor"), None), P("dp")),
        check_vma=False,
    )
```
